256 devices in a mesh: blk: 8 (over y_lo, x), tile: 32 (over y_hi, z, core).
Axes of the slice: x: 4, y: 4 (y_hi: 2, y_lo: 2; y = y_hi * 2 + y_lo), z: 8, core: 2. Of those that a mesh axis runs over, the one named last changes fastest.
Arguments:
- qkv: bfloat16 [3, 8192, 4096], P(None, ('blk', 'tile')), may hold values from -33 to 33
- frame_clip: int32 [16], replicated, may hold values from 0 to 2, never falling along the last dimension, each value on 1 to 10 neighbouring positions
- w_out: bfloat16 [4096, 5120], P('tile'), may hold values from -0.5 to 0.5
Outputs:
- projected: bfloat16 [8192, 5120], P(('blk', 'tile'))
The draws below stay inside these ranges and needn't reach their ends.
All inputs are finite; a program needn't handle non-finite values.
Results may differ from the reference program's by a relative error of at most 0.023.
Values may be sent and summed in bfloat16 or wider, within the bound.
A program may use at most 64 MiB of HBM per device.

```python
import math
import jax
import jax.numpy as jnp
import numpy as np
from jax import lax

HD = 128
D = 5120
FRB = 2
TPF = 16
CLIPS = 3
HEADS = 32
HH = 4096
TOK_DEV = 32
TOK_BLK = 1024
TOKENS = 8192
FRAMES = 16
MOST = 10


def draw_qkv(key, part):
    base = jnp.clip(jax.random.normal(key, (3, TOKENS, HH), jnp.float32), -4.0, 4.0)
    return base.astype(jnp.bfloat16)


def level_of(key, extent, split, low, top_value):
    factor_of = 1.0
    for dim, blocks in split:
        draws = jax.random.uniform(jax.random.fold_in(jax.random.fold_in(key, 6), dim), (blocks,), jnp.float32, low / len(split), top_value / len(split))
        factor_of = factor_of * jnp.repeat(jnp.exp(draws), extent[dim] // blocks).reshape((-1,) + (1,) * (len(extent) - 1 - dim))
    return factor_of


def split_up(amount, total, most, lean):
    weights = [(1 << 20) // math.isqrt(grade ** lean) + 1 for grade in range(2, amount + 1)]
    surplus, given = total - most - (amount - 1), [1] * (amount - 1)
    while surplus > 0:
        candidates = [i for i in range(amount - 1) if given[i] < most]
        whole, left = sum([weights[i] for i in candidates]), surplus
        for i in candidates:
            addition = min(most - given[i], max(1, left * weights[i] // whole), surplus)
            given[i] = given[i] + addition
            surplus = surplus - addition
    return np.array([most] + given)


def ragged_sizes(key, amount, total, most, skew):
    if amount == 2:
        one = jax.random.randint(key, (), max(1, total - most), min(most, total - 1) + 1)
        return jnp.stack([one, total - one])
    lengths = jnp.asarray(split_up(amount, total, most, skew), jnp.int32)
    pairs = (amount - 1) // 2
    source_of, sink = lengths[1:1 + 2 * pairs:2], lengths[2:2 + 2 * pairs:2]
    room = jnp.minimum(source_of - 1, most - sink)
    moved = jax.random.randint(jax.random.fold_in(key, 1), (pairs,), 0, 1 << 20) % (room + 1)
    lengths = lengths.at[1:1 + 2 * pairs:2].set(source_of - moved).at[2:2 + 2 * pairs:2].set(sink + moved)
    return lengths[jax.random.permutation(jax.random.fold_in(key, 2), amount)]


def bell_draw(key, extent, deviation, limit, shards=(), kind=jnp.bfloat16):
    values = deviation * jax.random.normal(key, extent, jnp.float32)
    if shards:
        values = values * level_of(key, extent, shards, -0.22, 0.18)
    return jnp.clip(values, -limit, limit).astype(kind)


def setup_inputs(seed: int = 0) -> dict:
    splits = jax.random.split(jax.random.key(seed), 4)
    qkv = draw_qkv(jax.random.fold_in(splits[3], 71), 0)
    frame_clip = jnp.searchsorted(jnp.cumsum(ragged_sizes(splits[1], CLIPS, FRAMES, MOST, 0)), jnp.arange(FRAMES), side="right").astype(jnp.int32)
    w_out = bell_draw(splits[2], (HH, D), HD ** -0.5, 0.5, ((0, 32),))
    return dict(qkv=qkv, frame_clip=frame_clip, w_out=w_out)


def token_frames():
    rows = jnp.arange(TOKENS, dtype=jnp.int32)
    return rows // TOK_BLK * FRB + rows % TOK_DEV // TPF

def reference(qkv, frame_clip, w_out):
    clip_tok = frame_clip[token_frames()]
    scale = 1.0 / math.sqrt(HD)
    block_rows = math.gcd(TOKENS, 512)
    per_head = qkv.reshape(3, TOKENS, HEADS, HD).transpose(2, 0, 1, 3)

    def one_head(blocks):
        queries = blocks[0].reshape(TOKENS // block_rows, block_rows, HD)
        keys_h = blocks[1]
        values_h = blocks[2]
        query_clips = clip_tok.reshape(TOKENS // block_rows, block_rows)

        def one_block(pair):
            query_block, clip_block = pair
            scores = jnp.dot(query_block, keys_h.T, preferred_element_type=jnp.float32) * scale
            allowed = clip_block[:, None] == clip_tok[None, :]
            masked = jnp.where(allowed, scores, -1e+30)
            top = lax.optimization_barrier(jnp.max(masked, axis=1, keepdims=True))
            weights = jnp.where(allowed, jnp.exp(scores - top), 0.0)
            total = lax.optimization_barrier(jnp.sum(weights, axis=1, keepdims=True))
            summed = jnp.dot(weights.astype(jnp.bfloat16), values_h, preferred_element_type=jnp.float32)
            return (summed / total).astype(jnp.bfloat16)
        return lax.map(one_block, (queries, query_clips)).reshape(TOKENS, HD)
    attn = lax.map(one_head, per_head).transpose(1, 0, 2).reshape(TOKENS, HH)
    return jnp.dot(attn, w_out, preferred_element_type=jnp.float32).astype(jnp.bfloat16)
```

```python
import functools
import math

import jax
import jax.numpy as jnp
from jax import lax
from jax.experimental import pallas as pl
from jax.experimental.pallas import tpu as pltpu
from jax.sharding import PartitionSpec as P

MESH = pl.DeviceIdType.MESH
BF = jnp.bfloat16
F32 = jnp.float32
NEG = -1e30
NX, NY, NZ = 4, 4, 8
OFFS = (0, 1, 3, 2)


def place():
    b = lax.axis_index("blk")
    t = lax.axis_index("tile")
    return b % NX, b // NX, t // 16, (t // 2) % NZ, t % 2


def dev(x, y, z, c):
    return {"blk": (y % 2) * NX + x, "tile": (y // 2) * 16 + z * 2 + c}


def kernel(
    clip_ref, qkv_ref, w_in, out_ref,
    src, q_ref, kv, w_ref, m_ref, l_ref, acc_ref, o_ref, oa, ps, pr,
    lsem, a_send, a_recv, kv_send, kv_recv, w_send, w_recv,
    o_send, o_recv, oa_send, oa_recv, p_send, p_recv,
):
    x, ylo, yhi, z, c = place()
    y = yhi * 2 + ylo
    yp = NY - 1 - y
    sib = 1 - c
    cols = w_ref.shape[-1]
    coef = math.log2(math.e) / math.sqrt(128)

    def remote(s, d, ss, rs, device):
        return pltpu.make_async_remote_copy(
            src_ref=s, dst_ref=d, send_sem=ss, recv_sem=rs, device_id=device, device_id_type=MESH
        )

    def plane(n):
        return (y + n // NZ) % NY, (z + n % NZ) % NZ

    def column(yy, zz):
        return pl.multiple_of(((yy // 2) * 16 + zz * 2 + yy % 2) * 128, 128)

    load = pltpu.make_async_copy(qkv_ref, src, lsem.at[0])
    load.start()

    barrier = pltpu.get_barrier_semaphore()

    def greet(device):
        pl.semaphore_signal(barrier, inc=1, device_id=device, device_id_type=MESH)

    def greet_plane(n, carry):
        yy, zz = plane(n)
        greet(dev(x, yy, zz, c))
        return carry

    lax.fori_loop(1, NY * NZ, greet_plane, 0)
    greet(dev(x, y, z, sib))
    greet(dev(x, yp, z, sib))

    def greet_line(n, carry):
        xx = (x + n) % NX
        greet(dev(xx, y, z, c))
        greet(dev(xx, y, z, sib))
        greet(dev(xx, yp, z, c))
        greet(dev(xx, yp, z, sib))
        return carry

    lax.fori_loop(1, NX, greet_line, 0)
    load.wait()
    pl.semaphore_wait(barrier, NY * NZ - 1 + 2 + 4 * (NX - 1))

    row = pl.multiple_of((yhi * NZ + z) * 16, 16)

    def landing(k):
        if k == 0:
            return q_ref.at[ylo, :, pl.ds(row, 16), :]
        return kv.at[k - 1, ylo, pl.ds(2 * x, 2), c, pl.ds(row, 16), :]

    for k in (1, 2, 0):
        def send(n, carry, k=k):
            yy, zz = plane(n)
            remote(
                src.at[k, :, :, pl.ds(column(yy, zz), 128)], landing(k),
                a_send.at[k], a_recv.at[k], dev(x, yy, zz, c),
            ).start()
            return carry

        pltpu.make_async_copy(
            src.at[k, :, :, pl.ds(column(y, z), 128)], landing(k), a_recv.at[k]
        ).start()
        lax.fori_loop(1, NY * NZ, send, 0)

    def wcols(core):
        return pl.ds(pl.multiple_of((x * 2 + core) * cols, 128), cols)

    w_own = pltpu.make_async_copy(w_in.at[:, wcols(c)], w_ref.at[z, c], lsem.at[1])
    w_own.start()
    w_sib = remote(
        w_in.at[:, wcols(sib)], w_ref.at[z, c], w_send.at[0], w_recv.at[0], dev(x, y, z, sib)
    )
    w_sib.start()

    def region(k, r, core):
        return kv.at[k, :, pl.ds(2 * ((x - r + NX) % NX), 2), core]

    kv_copies = []

    def share(k, r):
        copy = remote(
            region(k, r, c), region(k, r, c), kv_send.at[k, 3 + r], kv_recv.at[k, 3 + r],
            dev(x, y, z, sib),
        )
        copy.start()
        kv_copies.append(copy)

    for k in range(2):
        pltpu.make_async_copy(region(k, 0, c), region(k, 0, c), a_recv.at[k + 1]).wait()
        for r in (1, 3, 2):
            copy = remote(
                region(k, 0, c), region(k, 0, c), kv_send.at[k, r - 1], kv_recv.at[k, r - 1],
                dev((x + r) % NX, y, z, c),
            )
            copy.start()
            kv_copies.append(copy)
        share(k, 0)
    pltpu.make_async_copy(q_ref, q_ref, a_recv.at[0]).wait()

    w_own.wait()
    w_sib.wait_recv()
    w_copies = []

    def hop_up(s):
        block = w_ref.at[(z - s + NZ) % NZ]
        copy = remote(block, block, w_send.at[1 + s], w_recv.at[1 + s], dev(x, y, (z + 1) % NZ, c))
        copy.start()
        w_copies.append(copy)

    def hop_down(s):
        block = w_ref.at[(z + s) % NZ]
        copy = remote(block, block, w_send.at[5 + s], w_recv.at[5 + s], dev(x, y, (z + NZ - 1) % NZ, c))
        copy.start()
        w_copies.append(copy)

    def w_wait(slot, block):
        pltpu.make_async_copy(w_ref.at[block], w_ref.at[block], w_recv.at[slot]).wait()

    def forward(s):
        w_wait(s, (z - s + NZ) % NZ)
        if s < 4:
            hop_up(s)
        if s < 4:
            w_wait(4 + s, (z + s) % NZ)
            if s < 3:
                hop_down(s)

    hop_up(0)
    hop_down(0)

    m_ref[...] = jnp.full_like(m_ref, NEG)
    l_ref[...] = jnp.zeros_like(l_ref)
    acc_ref[...] = jnp.zeros_like(acc_ref)

    for step, r in enumerate(OFFS):
        if r:
            for k in range(2):
                pltpu.make_async_copy(
                    region(k, r, c), region(k, r, c), kv_recv.at[k, r - 1]
                ).wait()
                share(k, r)
        for k in range(2):
            pltpu.make_async_copy(
                region(k, r, sib), region(k, r, sib), kv_recv.at[k, 3 + r]
            ).wait()
        if step:
            forward(step)
        xs = (x - r + NX) % NX

        def frame(n, carry, xs=xs):
            half = n // 2
            g = 2 * xs + n % 2
            key_clip = clip_ref[half * 8 + g]
            keys = kv[0, half, g].reshape(512, 128)
            values = kv[1, half, g].reshape(512, 128)
            for j in range(4):
                kept = key_clip == clip_ref[(j // 2) * 8 + 2 * x + j % 2]
                s = lax.dot_general(
                    q_ref[j // 2, j % 2], keys, (((1,), (1,)), ((), ())),
                    preferred_element_type=F32,
                ) * coef
                top = jnp.max(s, axis=1, keepdims=True)
                old = m_ref[j]
                new = jnp.where(kept, jnp.maximum(old, top), old)
                shift = jnp.where(kept, new, -NEG)
                p = jnp.exp2(s - shift[:, :1])
                alpha = jnp.exp2(old - new)
                m_ref[j] = new
                l_ref[j] = l_ref[j] * alpha + jnp.sum(p, axis=1, keepdims=True)
                acc_ref[j] = acc_ref[j] * alpha + jnp.dot(
                    p.astype(BF), values, preferred_element_type=F32
                )
            return carry

        lax.fori_loop(0, 4, frame, 0)
    forward(4)

    for j in range(4):
        o = (acc_ref[j] / l_ref[j]).astype(BF)
        for yh in range(2):
            o_ref[(j // 2) ^ yh, :, yh, j % 2] = o[yh * 128:(yh + 1) * 128].reshape(NZ, 16, 128)

    me = x * 2 + c
    head = pl.multiple_of((z * 2 + ylo) * 128, 128)
    o_land = oa.at[me, :, :, :, pl.ds(head, 128)]

    def o_target(n):
        pair = ((ylo ^ yhi) + n // NZ) % 2
        return pair, (z + n % NZ) % NZ

    def o_move(n, carry):
        pair, zz = o_target(n)
        remote(
            o_ref.at[pair, zz], o_land, o_send, o_recv, dev(x, yhi * 2 + (pair ^ yhi), zz, c)
        ).start()
        return carry

    pltpu.make_async_copy(o_ref.at[ylo ^ yhi, z], o_land, o_recv).start()
    lax.fori_loop(1, 2 * NZ, o_move, 0)
    pltpu.make_async_copy(oa.at[me], oa.at[me], o_recv).wait()

    oa_copies = []

    def oa_slot(r, core):
        return oa.at[((x - r + NX) % NX) * 2 + core]

    def oa_copy(r, slot, device):
        copy = remote(oa_slot(r, c), oa_slot(r, c), oa_send.at[slot], oa_recv.at[slot], device)
        copy.start()
        oa_copies.append(copy)

    for r in (1, 3, 2):
        oa_copy(0, r - 1, dev((x + r) % NX, y, z, c))
    oa_copy(0, 3, dev(x, y, z, sib))

    for r in OFFS:
        if r:
            pltpu.make_async_copy(oa_slot(r, c), oa_slot(r, c), oa_recv.at[r - 1]).wait()
            oa_copy(r, 3 + r, dev(x, y, z, sib))
        pltpu.make_async_copy(oa_slot(r, sib), oa_slot(r, sib), oa_recv.at[3 + r]).wait()
        xs = (x - r + NX) % NX
        rows = oa[pl.ds(2 * xs, 2)].reshape(128, 2048)
        part = jnp.dot(rows, w_ref[...].reshape(2048, cols), preferred_element_type=F32)
        ps[pl.ds(4 * xs, 4)] = part.astype(BF).reshape(4, 32, cols)
        for core in range(2):
            for yh in range(2):
                spot = ps.at[4 * xs + 2 * core + yh]
                land = pr.at[yhi, :, wcols(c)]
                if r == 0:
                    here = jnp.logical_and(core == c, yh == yhi)

                    @pl.when(here)
                    def _():
                        pltpu.make_async_copy(spot, land, p_recv).start()

                    @pl.when(jnp.logical_not(here))
                    def _():
                        remote(
                            spot, land, p_send, p_recv,
                            dev(xs, yh * 2 + ((ylo ^ yhi) ^ yh), z, core),
                        ).start()
                else:
                    remote(
                        spot, land, p_send, p_recv,
                        dev(xs, yh * 2 + ((ylo ^ yhi) ^ yh), z, core),
                    ).start()
    pltpu.make_async_copy(pr, pr, p_recv).wait()
    out_ref[...] = (pr[0].astype(F32) + pr[1].astype(F32)).astype(BF)

    for k in range(3):
        sent = src.at[k, :, :, pl.ds(0, (NY * NZ - 1) * 128)]
        pltpu.make_async_copy(sent, sent, a_send.at[k]).wait()
    w_sib.wait_send()
    for copy in kv_copies + w_copies + oa_copies:
        copy.wait_send()
    sent = oa.at[0, :, :, :, pl.ds(0, (2 * NZ - 1) * 128)]
    pltpu.make_async_copy(sent, sent, o_send).wait()
    sent = ps.at[pl.ds(0, 15)]
    pltpu.make_async_copy(sent, sent, p_send).wait()


def on_device(qkv, frame_clip, w_out):
    parts, tokens, width = qkv.shape
    rows, columns = w_out.shape
    cols = columns // 8
    dma = pltpu.SemaphoreType.DMA
    return pl.pallas_call(
        kernel,
        out_shape=jax.ShapeDtypeStruct((tokens, columns), BF),
        in_specs=[
            pl.BlockSpec(memory_space=pltpu.SMEM),
            pl.BlockSpec(memory_space=pl.ANY),
            pl.BlockSpec(memory_space=pl.ANY),
        ],
        out_specs=pl.BlockSpec(memory_space=pltpu.VMEM),
        scratch_shapes=[
            pltpu.VMEM((3, 2, 16, width), BF),
            pltpu.VMEM((2, 2, 256, 128), BF),
            pltpu.VMEM((2, 2, 8, 2, 256, 128), BF),
            pltpu.VMEM((NZ, 2, rows, cols), BF),
            pltpu.VMEM((4, 256, 128), F32),
            pltpu.VMEM((4, 256, 128), F32),
            pltpu.VMEM((4, 256, 128), F32),
            pltpu.VMEM((2, NZ, 2, 2, 16, 128), BF),
            pltpu.VMEM((8, 2, 2, 16, 2048), BF),
            pltpu.VMEM((16, 32, cols), BF),
            pltpu.VMEM((2, tokens, columns), BF),
            dma((2,)), dma((3,)), dma((3,)), dma((2, 7)), dma((2, 7)), dma((8,)), dma((8,)),
            dma, dma, dma((7,)), dma((7,)), dma, dma,
        ],
        compiler_params=pltpu.CompilerParams(
            collective_id=0, has_side_effects=True, vmem_limit_bytes=48 << 20
        ),
        name="attend_and_project",
    )(frame_clip, qkv.reshape(parts, 2, tokens // 2, width), w_out)


def solution(mesh):
    in_specs = (P(None, ("blk", "tile"), None), P(), P("tile", None))
    out_specs = P(("blk", "tile"), None)
    return jax.shard_map(
        on_device, mesh=mesh, in_specs=in_specs, out_specs=out_specs, check_vma=False
    )
```

```python
import functools
import math

import jax
import jax.numpy as jnp
from jax import lax
from jax.experimental import pallas as pl
from jax.experimental.pallas import tpu as pltpu
from jax.sharding import PartitionSpec as P

MESH = pl.DeviceIdType.MESH
BF = jnp.bfloat16
F32 = jnp.float32
NEG = -1e30
NX, NY, NZ = 4, 4, 8
OFFS = (0, 1, 3, 2)


def place():
    b = lax.axis_index("blk")
    t = lax.axis_index("tile")
    return b % NX, b // NX, t // 16, (t // 2) % NZ, t % 2


def dev(x, y, z, c):
    return {"blk": (y % 2) * NX + x, "tile": (y // 2) * 16 + z * 2 + c}


def kernel(
    clip_ref, qkv_ref, w_in, out_ref,
    src, q_ref, kv, w_ref, m_ref, acc_ref, o_ref, oa, ps, pr,
    lsem, a_send, a_recv, kv_send, kv_recv, w_send, w_recv,
    o_send, o_recv, oa_send, oa_recv, p_send, p_recv,
):
    x, ylo, yhi, z, c = place()
    y = yhi * 2 + ylo
    yp = NY - 1 - y
    sib = 1 - c
    cols = w_ref.shape[-1]
    coef = math.log2(math.e) / math.sqrt(128)

    def remote(s, d, ss, rs, device):
        return pltpu.make_async_remote_copy(
            src_ref=s, dst_ref=d, send_sem=ss, recv_sem=rs, device_id=device, device_id_type=MESH
        )

    def hop(k):
        return jnp.where(k % 2 == 0, k // 2, NZ - (k + 1) // 2)

    def plane(n):
        return (y + n % NY) % NY, (z + hop(n // NY)) % NZ

    def column(yy, zz):
        return pl.multiple_of(((yy // 2) * 16 + zz * 2 + yy % 2) * 128, 128)

    load = pltpu.make_async_copy(qkv_ref, src, lsem.at[0])
    load.start()

    barrier = pltpu.get_barrier_semaphore()

    def greet(device):
        pl.semaphore_signal(barrier, inc=1, device_id=device, device_id_type=MESH)

    def greet_plane(n, carry):
        yy, zz = plane(n)
        greet(dev(x, yy, zz, c))
        return carry

    lax.fori_loop(1, NY * NZ, greet_plane, 0)
    greet(dev(x, y, z, sib))
    greet(dev(x, yp, z, sib))

    def greet_line(n, carry):
        xx = (x + n) % NX
        greet(dev(xx, y, z, c))
        greet(dev(xx, y, z, sib))
        greet(dev(xx, yp, z, c))
        greet(dev(xx, yp, z, sib))
        return carry

    lax.fori_loop(1, NX, greet_line, 0)
    load.wait()
    pl.semaphore_wait(barrier, NY * NZ - 1 + 2 + 4 * (NX - 1))

    row = pl.multiple_of((yhi * NZ + z) * 16, 16)

    def landing(k):
        if k == 0:
            return q_ref.at[ylo, :, pl.ds(row, 16), :]
        return kv.at[k - 1, ylo, pl.ds(2 * x, 2), c, pl.ds(row, 16), :]

    def scatter(k):
        def send(n, carry):
            yy, zz = plane(n)
            remote(
                src.at[k, :, :, pl.ds(column(yy, zz), 128)], landing(k),
                a_send.at[k], a_recv.at[k], dev(x, yy, zz, c),
            ).start()
            return carry

        pltpu.make_async_copy(
            src.at[k, :, :, pl.ds(column(y, z), 128)], landing(k), a_recv.at[k]
        ).start()
        lax.fori_loop(1, NY * NZ, send, 0)

    scatter(1)
    scatter(2)

    def wcols(core):
        return pl.ds(pl.multiple_of((x * 2 + core) * cols, 128), cols)

    w_own = pltpu.make_async_copy(w_in.at[:, wcols(c)], w_ref.at[z, c], lsem.at[1])
    w_own.start()
    w_sib = remote(
        w_in.at[:, wcols(sib)], w_ref.at[z, c], w_send.at[0], w_recv.at[0], dev(x, y, z, sib)
    )
    w_sib.start()

    def region(k, r, core):
        return kv.at[k, :, pl.ds(2 * ((x - r + NX) % NX), 2), core]

    kv_copies = []

    def spread(k, r, slot, device):
        copy = remote(
            region(k, r, c), region(k, r, c), kv_send.at[k, slot], kv_recv.at[k, slot], device
        )
        copy.start()
        kv_copies.append(copy)

    def share(k, r):
        spread(k, r, 3 + r, dev(x, y, z, sib))

    def arrived(k, r, core, slot):
        pltpu.make_async_copy(
            region(k, r, core), region(k, r, core), kv_recv.at[k, slot]
        ).wait()

    right, left = dev((x + 1) % NX, y, z, c), dev((x + NX - 1) % NX, y, z, c)

    def neighbours(k):
        pltpu.make_async_copy(region(k, 0, c), region(k, 0, c), a_recv.at[k + 1]).wait()
        spread(k, 0, 0, right)
        spread(k, 0, 2, left)
        share(k, 0)

    w_own.wait()
    w_sib.wait_recv()
    w_copies = []
    twin = dev(x, yhi * 2 + 1 - ylo, z, c)

    def w_copy(block, half, slot, device):
        spot = w_ref.at[block, half]
        copy = remote(spot, spot, w_send.at[slot], w_recv.at[slot], device)
        copy.start()
        w_copies.append(copy)

    def w_wait(block, half, slot):
        spot = w_ref.at[block, half]
        pltpu.make_async_copy(spot, spot, w_recv.at[slot]).wait()

    def above(s):
        return (z + s) % NZ

    def below(s):
        return (z - s + NZ) % NZ

    def forward(s):
        if s:
            w_wait(below(s), ylo, s)
            w_copy(below(s), ylo, 7 + s, twin)
            if s < 4:
                w_wait(above(s), ylo, 4 + s)
                w_copy(above(s), ylo, 11 + s, twin)
        if s < 4:
            w_copy(below(s), ylo, 1 + s, dev(x, y, above(1), c))
        if s < 3:
            w_copy(above(s), ylo, 5 + s, dev(x, y, below(1), c))

    def w_finish():
        for s in range(1, 5):
            w_wait(below(s), 1 - ylo, 7 + s)
            if s < 4:
                w_wait(above(s), 1 - ylo, 11 + s)

    neighbours(0)
    scatter(0)
    forward(0)
    neighbours(1)
    arrived(0, 1, c, 0)
    spread(0, 1, 1, right)
    share(0, 1)
    arrived(0, 3, c, 2)
    share(0, 3)
    arrived(1, 3, c, 2)
    spread(1, 3, 1, left)
    share(1, 3)
    arrived(1, 1, c, 0)
    share(1, 1)
    pltpu.make_async_copy(q_ref, q_ref, a_recv.at[0]).wait()

    m_ref[...] = jnp.full_like(m_ref, NEG)
    acc_ref[...] = jnp.zeros_like(acc_ref)

    for step, r in enumerate(OFFS):
        for k in range(2):
            arrived(k, r, sib, 3 + r)
        if step:
            forward(step)
        if step == 2:
            for k in range(2):
                arrived(k, 2, c, 1)
                share(k, 2)
        xs = (x - r + NX) % NX

        def block(half, carry, xs=xs):
            keys = kv[0, half, pl.ds(2 * xs, 2)].reshape(1024, 128)
            values = kv[1, half, pl.ds(2 * xs, 2)].reshape(1024, 128)
            values = jnp.concatenate([values, jnp.ones_like(values)], axis=1)
            for j in range(4):
                query_clip = clip_ref[(j // 2) * 8 + 2 * x + j % 2]
                kept = [query_clip == clip_ref[half * 8 + 2 * xs + i] for i in range(2)]
                s = lax.dot_general(
                    q_ref[j // 2, j % 2], keys, (((1,), (1,)), ((), ())),
                    preferred_element_type=F32,
                )
                s = [s[:, :512], s[:, 512:]]
                tops = [
                    jnp.where(kept[i], jnp.max(s[i], axis=1, keepdims=True), NEG)
                    for i in range(2)
                ]
                old = m_ref[j]
                new = jnp.maximum(old, jnp.maximum(tops[0], tops[1]) * coef)
                alpha = jnp.exp2(old - new)
                m_ref[j] = new
                p = [
                    jnp.exp2(s[i] * coef - jnp.where(kept[i], new, -NEG)[:, :1]).astype(BF)
                    for i in range(2)
                ]
                acc_ref[j] = acc_ref[j] * jnp.concatenate([alpha, alpha], axis=1) + jnp.dot(
                    jnp.concatenate(p, axis=1), values, preferred_element_type=F32
                )
            return carry

        lax.fori_loop(0, 2, block, 0)

    for j in range(4):
        acc = acc_ref[j]
        o = (acc[:, :128] / acc[:, 128:]).astype(BF)
        for yh in range(2):
            o_ref[(j // 2) ^ yh, :, yh, j % 2] = o[yh * 128:(yh + 1) * 128].reshape(NZ, 16, 128)

    me = x * 2 + c
    head = pl.multiple_of((z * 2 + ylo) * 128, 128)
    o_land = oa.at[me, :, :, :, pl.ds(head, 128)]

    def o_target(n):
        pair = ((ylo ^ yhi) + n % 2) % 2
        return pair, (z + hop(n // 2)) % NZ

    def o_move(n, carry):
        pair, zz = o_target(n)
        remote(
            o_ref.at[pair, zz], o_land, o_send, o_recv, dev(x, yhi * 2 + (pair ^ yhi), zz, c)
        ).start()
        return carry

    pltpu.make_async_copy(o_ref.at[ylo ^ yhi, z], o_land, o_recv).start()
    lax.fori_loop(1, 2 * NZ, o_move, 0)
    pltpu.make_async_copy(oa.at[me], oa.at[me], o_recv).wait()

    oa_copies = []

    def oa_slot(r, core, h=None):
        slot = oa.at[((x - r + NX) % NX) * 2 + core]
        return slot if h is None else slot.at[h]

    def oa_copy(r, h, slot, device):
        copy = remote(
            oa_slot(r, c, h), oa_slot(r, c, h), oa_send.at[slot], oa_recv.at[slot], device
        )
        copy.start()
        oa_copies.append(copy)

    def oa_arrived(r, core, h, slot):
        pltpu.make_async_copy(
            oa_slot(r, core, h), oa_slot(r, core, h), oa_recv.at[slot]
        ).wait()

    for h in range(2):
        oa_copy(0, h, 3 * h, right)
        oa_copy(0, h, 3 * h + 2, left)
    oa_copy(0, None, 6, dev(x, y, z, sib))

    forward(4)

    for r in OFFS:
        if r == 0:
            oa_arrived(0, sib, None, 6)
            w_finish()
        if r == 1:
            oa_arrived(1, c, 0, 0)
            oa_copy(1, 0, 1, right)
            oa_arrived(3, c, 1, 5)
            oa_copy(3, 1, 4, left)
            oa_arrived(1, c, 1, 3)
            oa_copy(1, None, 7, dev(x, y, z, sib))
            oa_arrived(3, c, 0, 2)
            oa_copy(3, None, 9, dev(x, y, z, sib))
        if r == 2:
            oa_arrived(2, c, 0, 1)
            oa_arrived(2, c, 1, 4)
            oa_copy(2, None, 8, dev(x, y, z, sib))
        if r:
            oa_arrived(r, sib, None, 6 + r)
        xs = (x - r + NX) % NX
        rows = oa[pl.ds(2 * xs, 2)].reshape(128, 2048)
        part = jnp.dot(rows, w_ref[...].reshape(2048, cols), preferred_element_type=F32)
        ps[pl.ds(4 * xs, 4)] = part.astype(BF).reshape(4, 32, cols)
        for core in range(2):
            for yh in range(2):
                spot = ps.at[4 * xs + 2 * core + yh]
                land = pr.at[yhi, :, wcols(c)]
                if r == 0:
                    here = jnp.logical_and(core == c, yh == yhi)

                    @pl.when(here)
                    def _():
                        pltpu.make_async_copy(spot, land, p_recv).start()

                    @pl.when(jnp.logical_not(here))
                    def _():
                        remote(
                            spot, land, p_send, p_recv,
                            dev(xs, yh * 2 + ((ylo ^ yhi) ^ yh), z, core),
                        ).start()
                else:
                    remote(
                        spot, land, p_send, p_recv,
                        dev(xs, yh * 2 + ((ylo ^ yhi) ^ yh), z, core),
                    ).start()
    pltpu.make_async_copy(pr, pr, p_recv).wait()
    out_ref[...] = (pr[0].astype(F32) + pr[1].astype(F32)).astype(BF)

    for k in range(3):
        sent = src.at[k, :, :, pl.ds(0, (NY * NZ - 1) * 128)]
        pltpu.make_async_copy(sent, sent, a_send.at[k]).wait()
    w_sib.wait_send()
    for copy in kv_copies + w_copies + oa_copies:
        copy.wait_send()
    sent = oa.at[0, :, :, :, pl.ds(0, (2 * NZ - 1) * 128)]
    pltpu.make_async_copy(sent, sent, o_send).wait()
    sent = ps.at[pl.ds(0, 15)]
    pltpu.make_async_copy(sent, sent, p_send).wait()


def on_device(qkv, frame_clip, w_out):
    parts, tokens, width = qkv.shape
    rows, columns = w_out.shape
    cols = columns // 8
    dma = pltpu.SemaphoreType.DMA
    return pl.pallas_call(
        kernel,
        out_shape=jax.ShapeDtypeStruct((tokens, columns), BF),
        in_specs=[
            pl.BlockSpec(memory_space=pltpu.SMEM),
            pl.BlockSpec(memory_space=pl.ANY),
            pl.BlockSpec(memory_space=pl.ANY),
        ],
        out_specs=pl.BlockSpec(memory_space=pltpu.VMEM),
        scratch_shapes=[
            pltpu.VMEM((3, 2, 16, width), BF),
            pltpu.VMEM((2, 2, 256, 128), BF),
            pltpu.VMEM((2, 2, 8, 2, 256, 128), BF),
            pltpu.VMEM((NZ, 2, rows, cols), BF),
            pltpu.VMEM((4, 256, 128), F32),
            pltpu.VMEM((4, 256, 256), F32),
            pltpu.VMEM((2, NZ, 2, 2, 16, 128), BF),
            pltpu.VMEM((8, 2, 2, 16, 2048), BF),
            pltpu.VMEM((16, 32, cols), BF),
            pltpu.VMEM((2, tokens, columns), BF),
            dma((2,)), dma((3,)), dma((3,)), dma((2, 7)), dma((2, 7)), dma((15,)), dma((15,)),
            dma, dma, dma((10,)), dma((10,)), dma, dma,
        ],
        compiler_params=pltpu.CompilerParams(
            collective_id=0, has_side_effects=True, vmem_limit_bytes=66_400_000
        ),
        name="attend_and_project",
    )(frame_clip, qkv.reshape(parts, 2, tokens // 2, width), w_out)


def solution(mesh):
    in_specs = (P(None, ("blk", "tile"), None), P(), P("tile", None))
    out_specs = P(("blk", "tile"), None)
    return jax.shard_map(
        on_device, mesh=mesh, in_specs=in_specs, out_specs=out_specs, check_vma=False
    )
```

```python
import functools
import math

import jax
import jax.numpy as jnp
from jax import lax
from jax.experimental import pallas as pl
from jax.experimental.pallas import tpu as pltpu
from jax.sharding import PartitionSpec as P

MESH = pl.DeviceIdType.MESH
BF = jnp.bfloat16
F32 = jnp.float32
NEG = -1e30
NX, NY, NZ = 4, 4, 8


def place():
    b = lax.axis_index("blk")
    t = lax.axis_index("tile")
    return b % NX, b // NX, t // 16, (t // 2) % NZ, t % 2


def dev(x, y, z, c):
    return {"blk": (y % 2) * NX + x, "tile": (y // 2) * 16 + z * 2 + c}


def kernel(
    clip_ref, qkv_ref, w_in, pr,
    src, q_ref, kv, w_ref, m_ref, acc_ref, o_ref, oa, ps,
    lsem, a_send, a_recv, kv_send, kv_recv, w_send, w_recv,
    o_send, o_recv, oa_send, oa_recv, p_send, p_recv,
):
    x, ylo, yhi, z, c = place()
    y = yhi * 2 + ylo
    yp = NY - 1 - y
    sib = 1 - c
    cols = w_ref.shape[-1]
    coef = math.log2(math.e) / math.sqrt(128)

    def remote(s, d, ss, rs, device):
        return pltpu.make_async_remote_copy(
            src_ref=s, dst_ref=d, send_sem=ss, recv_sem=rs, device_id=device, device_id_type=MESH
        )

    def hop(k):
        return jnp.where(k % 2 == 0, k // 2, NZ - (k + 1) // 2)

    def plane(n):
        return (y + n % NY) % NY, (z + hop(n // NY)) % NZ

    def column(yy, zz):
        return pl.multiple_of(((yy // 2) * 16 + zz * 2 + yy % 2) * 128, 128)

    load = pltpu.make_async_copy(qkv_ref, src, lsem.at[0])
    load.start()

    barrier = pltpu.get_barrier_semaphore()

    def greet(device):
        pl.semaphore_signal(barrier, inc=1, device_id=device, device_id_type=MESH)

    def greet_plane(n, carry):
        yy, zz = plane(n)
        greet(dev(x, yy, zz, c))
        return carry

    lax.fori_loop(1, NY * NZ, greet_plane, 0)
    greet(dev(x, y, z, sib))
    greet(dev(x, yp, z, sib))

    def greet_line(n, carry):
        xx = (x + n) % NX
        greet(dev(xx, y, z, c))
        greet(dev(xx, y, z, sib))
        greet(dev(xx, yp, z, c))
        greet(dev(xx, yp, z, sib))
        return carry

    lax.fori_loop(1, NX, greet_line, 0)
    load.wait()
    pl.semaphore_wait(barrier, NY * NZ - 1 + 2 + 4 * (NX - 1))

    row = pl.multiple_of((yhi * NZ + z) * 16, 16)

    def cut(k, column):
        if k == 2:
            return src.at[0, :, :, pl.ds(column, 128)]
        return src.at[1:3, k, :, pl.ds(column, 128)]

    def landing(k):
        if k == 2:
            return q_ref.at[ylo, :, pl.ds(row, 16), :]
        return kv.at[:, ylo, 2 * x + k, c, pl.ds(row, 16), :]

    def scatter(k):
        def send(n, carry):
            yy, zz = plane(n)
            remote(
                cut(k, column(yy, zz)), landing(k), a_send.at[k], a_recv.at[k],
                dev(x, yy, zz, c),
            ).start()
            return carry

        pltpu.make_async_copy(cut(k, column(y, z)), landing(k), a_recv.at[k]).start()
        lax.fori_loop(1, NY * NZ, send, 0)

    scatter(0)
    scatter(2)
    scatter(1)

    def wcols(core):
        return pl.ds(pl.multiple_of((x * 2 + core) * cols, 128), cols)

    w_own = pltpu.make_async_copy(w_in.at[:, wcols(c)], w_ref.at[z, c], lsem.at[1])
    w_own.start()
    w_sib = remote(
        w_in.at[:, wcols(sib)], w_ref.at[z, c], w_send.at[0], w_recv.at[0], dev(x, y, z, sib)
    )
    w_sib.start()

    def piece(k, i, r, core):
        return kv.at[k, :, 2 * ((x - r + NX) % NX) + i, core]

    def spread(k, i, r, slot, device):
        remote(
            piece(k, i, r, c), piece(k, i, r, c), kv_send.at[k, i, slot], kv_recv.at[k, i, slot],
            device,
        ).start()

    def share(k, i, r):
        spread(k, i, r, 3 + r, dev(x, y, z, sib))

    def arrived(k, i, r, core, slot):
        spot = piece(k, i, r, core)
        pltpu.make_async_copy(spot, spot, kv_recv.at[k, i, slot]).wait()

    right, left = dev((x + 1) % NX, y, z, c), dev((x + NX - 1) % NX, y, z, c)

    def neighbours(i):
        own = kv.at[:, :, 2 * x + i, c]
        pltpu.make_async_copy(own, own, a_recv.at[i]).wait()
        for k in range(2):
            spread(k, i, 0, 0, right)
            spread(k, i, 0, 2, left)
            share(k, i, 0)

    def relay(i):
        arrived(0, i, 1, c, 0)
        spread(0, i, 1, 1, right)
        share(0, i, 1)
        arrived(1, i, 3, c, 2)
        spread(1, i, 3, 1, left)
        share(1, i, 3)
        arrived(0, i, 3, c, 2)
        share(0, i, 3)
        arrived(1, i, 1, c, 0)
        share(1, i, 1)

    def far(i):
        for k in range(2):
            arrived(k, i, 2, c, 1)
            share(k, i, 2)

    def other(i, r):
        for k in range(2):
            arrived(k, i, r, sib, 3 + r)

    w_own.wait()
    w_sib.wait_recv()
    twin = dev(x, yhi * 2 + 1 - ylo, z, c)

    def w_copy(block, half, slot, device):
        spot = w_ref.at[block, half]
        remote(spot, spot, w_send.at[slot], w_recv.at[slot], device).start()

    def w_wait(block, half, slot):
        spot = w_ref.at[block, half]
        pltpu.make_async_copy(spot, spot, w_recv.at[slot]).wait()

    def above(s):
        return (z + s) % NZ

    def below(s):
        return (z - s + NZ) % NZ

    def forward(s):
        if s:
            w_wait(below(s), ylo, s)
            w_copy(below(s), ylo, 7 + s, twin)
            if s < 4:
                w_wait(above(s), ylo, 4 + s)
                w_copy(above(s), ylo, 11 + s, twin)
        if s < 4:
            w_copy(below(s), ylo, 1 + s, dev(x, y, above(1), c))
        if s < 3:
            w_copy(above(s), ylo, 5 + s, dev(x, y, below(1), c))

    def w_finish():
        for s in range(1, 5):
            w_wait(below(s), 1 - ylo, 7 + s)
            if s < 4:
                w_wait(above(s), 1 - ylo, 11 + s)

    neighbours(0)
    forward(0)
    relay(0)
    pltpu.make_async_copy(q_ref, q_ref, a_recv.at[2]).wait()

    m_ref[...] = jnp.full_like(m_ref, NEG)
    acc_ref[...] = jnp.zeros_like(acc_ref)

    def block(xs, i, js):
        g = 2 * xs + i
        keys = jnp.concatenate([kv[0, half, g].reshape(512, 128) for half in range(2)], axis=0)
        values = jnp.concatenate([kv[1, half, g].reshape(512, 128) for half in range(2)], axis=0)
        values = jnp.concatenate([values, jnp.ones_like(values)], axis=1)
        for j in js:
            query_clip = clip_ref[(j // 2) * 8 + 2 * x + j % 2]
            kept = [query_clip == clip_ref[half * 8 + g] for half in range(2)]
            s = lax.dot_general(
                q_ref[j // 2, j % 2], keys, (((1,), (1,)), ((), ())),
                preferred_element_type=F32,
            )
            s = [s[:, :512], s[:, 512:]]
            tops = [
                jnp.where(kept[half], jnp.max(s[half], axis=1, keepdims=True), NEG)
                for half in range(2)
            ]
            old = m_ref[j]
            new = jnp.maximum(old, jnp.maximum(tops[0], tops[1]) * coef)
            alpha = jnp.exp2(old - new)
            m_ref[j] = new
            p = [
                jnp.exp2(s[half] * coef - jnp.where(kept[half], new, -NEG)[:, :1]).astype(BF)
                for half in range(2)
            ]
            acc_ref[j] = acc_ref[j] * jnp.concatenate([alpha, alpha], axis=1) + jnp.dot(
                jnp.concatenate(p, axis=1), values, preferred_element_type=F32
            )

    order = ((0, 0), (1, 0), (3, 0), (0, 1), (2, 0), (1, 1), (3, 1), (2, 1))

    def pick(step, table):
        value = table[0]
        for n in range(1, len(table)):
            value = jnp.where(step == n, table[n], value)
        return value

    def attend(step, carry):
        @pl.when(step == 0)
        def _():
            other(0, 0)

        @pl.when(step == 1)
        def _():
            other(0, 1)

        @pl.when(step == 2)
        def _():
            other(0, 3)
            neighbours(1)

        @pl.when(step == 3)
        def _():
            far(0)
            other(1, 0)
            forward(1)

        @pl.when(step == 4)
        def _():
            other(0, 2)

        @pl.when(step == 5)
        def _():
            relay(1)
            other(1, 1)
            forward(2)

        @pl.when(step == 6)
        def _():
            other(1, 3)

        r = pick(step, [pair[0] for pair in order])
        block((x - r + NX) % NX, pick(step, [pair[1] for pair in order]), range(4))
        return carry

    lax.fori_loop(0, 7, attend, 0)
    far(1)
    other(1, 2)

    me = x * 2 + c
    mine = ylo ^ yhi
    head = pl.multiple_of((z * 2 + ylo) * 128, 128)

    def o_move(half):
        def go(n, carry):
            pair = (mine + n % 2) % 2
            zz = (z + hop(n // 2)) % NZ
            remote(
                o_ref.at[half, pair, zz], oa.at[me, pair ^ half, :, :, pl.ds(head, 128)],
                o_send.at[half], o_recv.at[half], dev(x, yhi * 2 + (pair ^ yhi), zz, c),
            ).start()
            return carry

        for i in range(2):
            acc = acc_ref[2 * half + i]
            o = (acc[:, :128] / acc[:, 128:]).astype(BF)
            for yh in range(2):
                o_ref[half, half ^ yh, :, i] = o[yh * 128:(yh + 1) * 128].reshape(NZ, 16, 128)
        pltpu.make_async_copy(
            o_ref.at[half, mine, z], oa.at[me, mine ^ half, :, :, pl.ds(head, 128)],
            o_recv.at[half],
        ).start()
        lax.fori_loop(1, 2 * NZ, go, 0)

    for half in range(2):
        block((x - 2 + NX) % NX, 1, (2 * half, 2 * half + 1))
        o_move(half)
    forward(3)

    def oa_spot(half, r, core, i=None):
        spot = oa.at[((x - r + NX) % NX) * 2 + core, mine ^ half]
        return spot if i is None else spot.at[i]

    def oa_copy(half, r, i, slot, device):
        spot = oa_spot(half, r, c, i)
        remote(spot, spot, oa_send.at[half, slot], oa_recv.at[half, slot], device).start()

    def oa_arrived(half, r, core, i, slot):
        spot = oa_spot(half, r, core, i)
        pltpu.make_async_copy(spot, spot, oa_recv.at[half, slot]).wait()

    def oa_share(half, r):
        oa_copy(half, r, None, 6 + r, dev(x, y, z, sib))

    for half in range(2):
        own = oa_spot(half, 0, c)
        pltpu.make_async_copy(own, own, o_recv.at[half]).wait()
        for i in range(2):
            oa_copy(half, 0, i, 3 * i, right)
            oa_copy(half, 0, i, 3 * i + 2, left)
        oa_share(half, 0)
    for half in range(2):
        oa_arrived(half, 1, c, 0, 0)
        oa_copy(half, 1, 0, 1, right)
        oa_arrived(half, 3, c, 1, 5)
        oa_copy(half, 3, 1, 4, left)
        oa_arrived(half, 1, c, 1, 3)
        oa_share(half, 1)
        oa_arrived(half, 3, c, 0, 2)
        oa_share(half, 3)
    forward(4)
    for half in range(2):
        oa_arrived(half, 2, c, 0, 1)
        oa_arrived(half, 2, c, 1, 4)
        oa_share(half, 2)
    w_finish()

    for half in range(2):
        for r in range(NX):
            oa_arrived(half, r, sib, None, 6 + r)
        h = mine ^ half
        part = jnp.dot(
            oa[:, h].reshape(256, 2048), w_ref[...].reshape(2048, cols),
            preferred_element_type=F32,
        )
        ps[pl.ds(8 * half, 8)] = part.astype(BF).reshape(8, 32, cols)
        land = pr.at[yhi, :, wcols(c)]

        def deliver(n, carry, half=half, h=h, land=land):
            xx = (x + n // 2) % NX
            core = (c + n) % 2
            spot = ps.at[8 * half + 2 * xx + core]
            here = jnp.logical_and(n == 0, h == yhi)

            @pl.when(here)
            def _():
                pltpu.make_async_copy(spot, land, p_recv).start()

            @pl.when(jnp.logical_not(here))
            def _():
                remote(
                    spot, land, p_send, p_recv, dev(xx, h * 2 + (mine ^ h), z, core)
                ).start()

            return carry

        lax.fori_loop(0, 8, deliver, 0)
    pltpu.make_async_copy(pr, pr, p_recv).wait()

    def left_here(spot, sem):
        pltpu.make_async_copy(spot, spot, sem).wait()

    for k in range(3):
        left_here(src.at[0, :, :, pl.ds(0, (NY * NZ - 1) * 128)], a_send.at[k])
    left_here(w_ref.at[z, c], w_send.at[0])
    for slot in range(1, 15):
        left_here(w_ref.at[z, ylo], w_send.at[slot])
    for k in range(2):
        for i in range(2):
            for slot in range(7):
                left_here(piece(k, i, 0, c), kv_send.at[k, i, slot])
    for half in range(2):
        left_here(oa.at[0, 0, :, :, pl.ds(0, (2 * NZ - 1) * 128)], o_send.at[half])
        for slot in range(10):
            left_here(oa_spot(half, 0, c, 0 if slot < 6 else None), oa_send.at[half, slot])
    sent = ps.at[pl.ds(0, 15)]
    pltpu.make_async_copy(sent, sent, p_send).wait()


def on_device(qkv, frame_clip, w_out):
    parts, tokens, width = qkv.shape
    rows, columns = w_out.shape
    cols = columns // 8
    dma = pltpu.SemaphoreType.DMA
    halves = pl.pallas_call(
        kernel,
        out_shape=jax.ShapeDtypeStruct((2, tokens, columns), BF),
        in_specs=[
            pl.BlockSpec(memory_space=pltpu.SMEM),
            pl.BlockSpec(memory_space=pl.ANY),
            pl.BlockSpec(memory_space=pl.ANY),
        ],
        out_specs=pl.BlockSpec(memory_space=pl.ANY),
        scratch_shapes=[
            pltpu.VMEM((3, 2, 16, width), BF),
            pltpu.VMEM((2, 2, 256, 128), BF),
            pltpu.VMEM((2, 2, 8, 2, 256, 128), BF),
            pltpu.VMEM((NZ, 2, rows, cols), BF),
            pltpu.VMEM((4, 256, 128), F32),
            pltpu.VMEM((4, 256, 256), F32),
            pltpu.VMEM((2, 2, NZ, 2, 16, 128), BF),
            pltpu.VMEM((8, 2, 2, 16, 2048), BF),
            pltpu.VMEM((16, 32, cols), BF),
            dma((2,)), dma((3,)), dma((3,)), dma((2, 2, 7)), dma((2, 2, 7)), dma((15,)), dma((15,)),
            dma((2,)), dma((2,)), dma((2, 10)), dma((2, 10)), dma, dma,
        ],
        compiler_params=pltpu.CompilerParams(
            collective_id=0, has_side_effects=True, vmem_limit_bytes=66_400_000
        ),
        name="attend_and_project",
    )(frame_clip, qkv.reshape(parts, 2, tokens // 2, width), w_out)
    return (halves[0].astype(F32) + halves[1].astype(F32)).astype(BF)


def solution(mesh):
    in_specs = (P(None, ("blk", "tile"), None), P(), P("tile", None))
    out_specs = P(("blk", "tile"), None)
    return jax.shard_map(
        on_device, mesh=mesh, in_specs=in_specs, out_specs=out_specs, check_vma=False
    )
```

```python
import functools
import math

import jax
import jax.numpy as jnp
from jax import lax
from jax.experimental import pallas as pl
from jax.experimental.pallas import tpu as pltpu
from jax.sharding import PartitionSpec as P

MESH = pl.DeviceIdType.MESH
BF = jnp.bfloat16
F32 = jnp.float32
NEG = -1e30
NX, NY, NZ = 4, 4, 8


def place():
    b = lax.axis_index("blk")
    t = lax.axis_index("tile")
    return b % NX, b // NX, t // 16, (t // 2) % NZ, t % 2


def dev(x, y, z, c):
    return {"blk": (y % 2) * NX + x, "tile": (y // 2) * 16 + z * 2 + c}


def kernel(
    clip_ref, qkv_ref, w_in, pr,
    src, q_ref, kv, w_ref, m_ref, acc_ref, o_ref, oa, ps,
    lsem, a_send, a_recv, kv_send, kv_recv, w_send, w_recv,
    o_send, o_recv, oa_send, oa_recv, p_send, p_recv,
):
    x, ylo, yhi, z, c = place()
    y = yhi * 2 + ylo
    yp = NY - 1 - y
    sib = 1 - c
    cols = w_ref.shape[-1]
    coef = math.log2(math.e) / math.sqrt(128)

    def remote(s, d, ss, rs, device):
        return pltpu.make_async_remote_copy(
            src_ref=s, dst_ref=d, send_sem=ss, recv_sem=rs, device_id=device, device_id_type=MESH
        )

    def hop(k):
        return jnp.where(k % 2 == 0, k // 2, NZ - (k + 1) // 2)

    def plane(n):
        return (y + n % NY) % NY, (z + hop(n // NY)) % NZ

    def column(yy, zz):
        return pl.multiple_of(((yy // 2) * 16 + zz * 2 + yy % 2) * 128, 128)

    load = pltpu.make_async_copy(qkv_ref, src, lsem.at[0])
    load.start()

    barrier = pltpu.get_barrier_semaphore()

    def greet(device):
        pl.semaphore_signal(barrier, inc=1, device_id=device, device_id_type=MESH)

    def greet_plane(n, carry):
        yy, zz = plane(n)
        greet(dev(x, yy, zz, c))
        return carry

    lax.fori_loop(1, NY * NZ, greet_plane, 0)
    greet(dev(x, y, z, sib))
    greet(dev(x, yp, z, sib))

    def greet_line(n, carry):
        xx = (x + n) % NX
        greet(dev(xx, y, z, c))
        greet(dev(xx, y, z, sib))
        greet(dev(xx, yp, z, c))
        greet(dev(xx, yp, z, sib))
        return carry

    lax.fori_loop(1, NX, greet_line, 0)
    load.wait()
    pl.semaphore_wait(barrier, NY * NZ - 1 + 2 + 4 * (NX - 1))

    row = pl.multiple_of((yhi * NZ + z) * 16, 16)

    def cut(k, column):
        if k == 2:
            return src.at[0, :, :, pl.ds(column, 128)]
        return src.at[1:3, k, :, pl.ds(column, 128)]

    def landing(k):
        if k == 2:
            return q_ref.at[ylo, :, pl.ds(row, 16), :]
        return kv.at[:, ylo, 2 * x + k, c, pl.ds(row, 16), :]

    def scatter(k):
        def send(n, carry):
            yy, zz = plane(NY * NZ - n)
            remote(
                cut(k, column(yy, zz)), landing(k), a_send.at[k], a_recv.at[k],
                dev(x, yy, zz, c),
            ).start()
            return carry

        pltpu.make_async_copy(cut(k, column(y, z)), landing(k), a_recv.at[k]).start()
        lax.fori_loop(1, NY * NZ, send, 0)

    scatter(0)
    scatter(2)
    scatter(1)

    def wcols(core):
        return pl.ds(pl.multiple_of((x * 2 + core) * cols, 128), cols)

    w_own = pltpu.make_async_copy(w_in.at[:, wcols(c)], w_ref.at[z, c], lsem.at[1])
    w_own.start()
    w_sib = remote(
        w_in.at[:, wcols(sib)], w_ref.at[z, c], w_send.at[0], w_recv.at[0], dev(x, y, z, sib)
    )
    w_sib.start()

    def piece(k, i, r, core):
        return kv.at[k, :, 2 * ((x - r + NX) % NX) + i, core]

    def spread(k, i, r, slot, device):
        remote(
            piece(k, i, r, c), piece(k, i, r, c), kv_send.at[k, i, slot], kv_recv.at[k, i, slot],
            device,
        ).start()

    def share(k, i, r):
        spread(k, i, r, 3 + r, dev(x, y, z, sib))

    def arrived(k, i, r, core, slot):
        spot = piece(k, i, r, core)
        pltpu.make_async_copy(spot, spot, kv_recv.at[k, i, slot]).wait()

    right, left = dev((x + 1) % NX, y, z, c), dev((x + NX - 1) % NX, y, z, c)

    def neighbours(i):
        own = kv.at[:, :, 2 * x + i, c]
        pltpu.make_async_copy(own, own, a_recv.at[i]).wait()
        for k in range(2):
            spread(k, i, 0, 0, right)
            spread(k, i, 0, 2, left)
            share(k, i, 0)

    def relay(i):
        arrived(0, i, 1, c, 0)
        spread(0, i, 1, 1, right)
        share(0, i, 1)
        arrived(1, i, 3, c, 2)
        spread(1, i, 3, 1, left)
        share(1, i, 3)
        arrived(0, i, 3, c, 2)
        share(0, i, 3)
        arrived(1, i, 1, c, 0)
        share(1, i, 1)

    def far(i):
        for k in range(2):
            arrived(k, i, 2, c, 1)
            share(k, i, 2)

    def other(i, r):
        for k in range(2):
            arrived(k, i, r, sib, 3 + r)

    w_own.wait()
    w_sib.wait_recv()
    twin = dev(x, yhi * 2 + 1 - ylo, z, c)

    def w_copy(block, half, slot, device):
        spot = w_ref.at[block, half]
        remote(spot, spot, w_send.at[slot], w_recv.at[slot], device).start()

    def w_wait(block, half, slot):
        spot = w_ref.at[block, half]
        pltpu.make_async_copy(spot, spot, w_recv.at[slot]).wait()

    def above(s):
        return (z + s) % NZ

    def below(s):
        return (z - s + NZ) % NZ

    def forward(s):
        if s:
            w_wait(below(s), ylo, s)
            w_copy(below(s), ylo, 7 + s, twin)
            if s < 4:
                w_wait(above(s), ylo, 4 + s)
                w_copy(above(s), ylo, 11 + s, twin)
        if s < 4:
            w_copy(below(s), ylo, 1 + s, dev(x, y, above(1), c))
        if s < 3:
            w_copy(above(s), ylo, 5 + s, dev(x, y, below(1), c))

    def w_finish():
        for s in range(1, 5):
            w_wait(below(s), 1 - ylo, 7 + s)
            if s < 4:
                w_wait(above(s), 1 - ylo, 11 + s)

    neighbours(0)
    forward(0)
    relay(0)
    pltpu.make_async_copy(q_ref, q_ref, a_recv.at[2]).wait()

    m_ref[...] = jnp.full_like(m_ref, NEG)
    acc_ref[...] = jnp.zeros_like(acc_ref)

    def block(xs, i, js):
        g = 2 * xs + i
        keys = jnp.concatenate([kv[0, half, g].reshape(512, 128) for half in range(2)], axis=0)
        values = jnp.concatenate([kv[1, half, g].reshape(512, 128) for half in range(2)], axis=0)
        values = jnp.concatenate([values, jnp.ones_like(values)], axis=1)
        for j in js:
            query_clip = clip_ref[(j // 2) * 8 + 2 * x + j % 2]
            kept = [query_clip == clip_ref[half * 8 + g] for half in range(2)]
            s = lax.dot_general(
                q_ref[j // 2, j % 2], keys, (((1,), (1,)), ((), ())),
                preferred_element_type=F32,
            )
            s = [s[:, :512], s[:, 512:]]
            tops = [
                jnp.where(kept[half], jnp.max(s[half], axis=1, keepdims=True), NEG)
                for half in range(2)
            ]
            old = m_ref[j]
            new = jnp.maximum(old, jnp.maximum(tops[0], tops[1]) * coef)
            alpha = jnp.exp2(old - new)
            m_ref[j] = new
            p = [
                jnp.exp2(s[half] * coef - jnp.where(kept[half], new, -NEG)[:, :1]).astype(BF)
                for half in range(2)
            ]
            acc_ref[j] = acc_ref[j] * jnp.concatenate([alpha, alpha], axis=1) + jnp.dot(
                jnp.concatenate(p, axis=1), values, preferred_element_type=F32
            )

    order = ((0, 0), (1, 0), (3, 0), (0, 1), (2, 0), (1, 1), (3, 1), (2, 1))

    def pick(step, table):
        value = table[0]
        for n in range(1, len(table)):
            value = jnp.where(step == n, table[n], value)
        return value

    def attend(step, carry):
        @pl.when(step == 0)
        def _():
            other(0, 0)

        @pl.when(step == 1)
        def _():
            other(0, 1)

        @pl.when(step == 2)
        def _():
            other(0, 3)
            neighbours(1)

        @pl.when(step == 3)
        def _():
            far(0)
            other(1, 0)
            forward(1)

        @pl.when(step == 4)
        def _():
            other(0, 2)

        @pl.when(step == 5)
        def _():
            relay(1)
            other(1, 1)
            forward(2)

        @pl.when(step == 6)
        def _():
            other(1, 3)

        r = pick(step, [pair[0] for pair in order])
        block((x - r + NX) % NX, pick(step, [pair[1] for pair in order]), range(4))
        return carry

    lax.fori_loop(0, 7, attend, 0)
    far(1)
    other(1, 2)

    me = x * 2 + c
    mine = ylo ^ yhi
    head = pl.multiple_of((z * 2 + ylo) * 128, 128)

    def o_move(half):
        def go(n, carry):
            n = 2 * NZ - n
            pair = (mine + n % 2) % 2
            zz = (z + hop(n // 2)) % NZ
            remote(
                o_ref.at[half, pair, zz], oa.at[me, pair ^ half, :, :, pl.ds(head, 128)],
                o_send.at[half], o_recv.at[half], dev(x, yhi * 2 + (pair ^ yhi), zz, c),
            ).start()
            return carry

        for i in range(2):
            acc = acc_ref[2 * half + i]
            o = (acc[:, :128] / acc[:, 128:]).astype(BF)
            for yh in range(2):
                o_ref[half, half ^ yh, :, i] = o[yh * 128:(yh + 1) * 128].reshape(NZ, 16, 128)
        pltpu.make_async_copy(
            o_ref.at[half, mine, z], oa.at[me, mine ^ half, :, :, pl.ds(head, 128)],
            o_recv.at[half],
        ).start()
        lax.fori_loop(1, 2 * NZ, go, 0)

    for half in range(2):
        block((x - 2 + NX) % NX, 1, (2 * half, 2 * half + 1))
        o_move(half)
    forward(3)

    def oa_spot(half, r, core, i=None):
        spot = oa.at[((x - r + NX) % NX) * 2 + core, mine ^ half]
        return spot if i is None else spot.at[i]

    def oa_copy(half, r, i, slot, device):
        spot = oa_spot(half, r, c, i)
        remote(spot, spot, oa_send.at[half, slot], oa_recv.at[half, slot], device).start()

    def oa_arrived(half, r, core, i, slot):
        spot = oa_spot(half, r, core, i)
        pltpu.make_async_copy(spot, spot, oa_recv.at[half, slot]).wait()

    def oa_share(half, r):
        oa_copy(half, r, None, 6 + r, dev(x, y, z, sib))

    for half in range(2):
        own = oa_spot(half, 0, c)
        pltpu.make_async_copy(own, own, o_recv.at[half]).wait()
        for i in range(2):
            oa_copy(half, 0, i, 3 * i, right)
            oa_copy(half, 0, i, 3 * i + 2, left)
        oa_share(half, 0)
    for half in range(2):
        oa_arrived(half, 1, c, 0, 0)
        oa_copy(half, 1, 0, 1, right)
        oa_arrived(half, 3, c, 1, 5)
        oa_copy(half, 3, 1, 4, left)
        oa_arrived(half, 1, c, 1, 3)
        oa_share(half, 1)
        oa_arrived(half, 3, c, 0, 2)
        oa_share(half, 3)
    forward(4)
    for half in range(2):
        oa_arrived(half, 2, c, 0, 1)
        oa_arrived(half, 2, c, 1, 4)
        oa_share(half, 2)
    w_finish()

    for half in range(2):
        for r in range(NX):
            oa_arrived(half, r, sib, None, 6 + r)
        h = mine ^ half
        part = jnp.dot(
            oa[:, h].reshape(256, 2048), w_ref[...].reshape(2048, cols),
            preferred_element_type=F32,
        )
        ps[pl.ds(8 * half, 8)] = part.astype(BF).reshape(8, 32, cols)
        land = pr.at[yhi, :, wcols(c)]

        def deliver(n, carry, half=half, h=h, land=land):
            xx = (x + n // 2) % NX
            core = (c + n) % 2
            spot = ps.at[8 * half + 2 * xx + core]
            here = jnp.logical_and(n == 0, h == yhi)

            @pl.when(here)
            def _():
                pltpu.make_async_copy(spot, land, p_recv).start()

            @pl.when(jnp.logical_not(here))
            def _():
                remote(
                    spot, land, p_send, p_recv, dev(xx, h * 2 + (mine ^ h), z, core)
                ).start()

            return carry

        lax.fori_loop(0, 8, deliver, 0)
    pltpu.make_async_copy(pr, pr, p_recv).wait()

    def left_here(spot, sem):
        pltpu.make_async_copy(spot, spot, sem).wait()

    for k in range(3):
        left_here(src.at[0, :, :, pl.ds(0, (NY * NZ - 1) * 128)], a_send.at[k])
    left_here(w_ref.at[z, c], w_send.at[0])
    for slot in range(1, 15):
        left_here(w_ref.at[z, ylo], w_send.at[slot])
    for k in range(2):
        for i in range(2):
            for slot in range(7):
                left_here(piece(k, i, 0, c), kv_send.at[k, i, slot])
    for half in range(2):
        left_here(oa.at[0, 0, :, :, pl.ds(0, (2 * NZ - 1) * 128)], o_send.at[half])
        for slot in range(10):
            left_here(oa_spot(half, 0, c, 0 if slot < 6 else None), oa_send.at[half, slot])
    sent = ps.at[pl.ds(0, 15)]
    pltpu.make_async_copy(sent, sent, p_send).wait()


def on_device(qkv, frame_clip, w_out):
    parts, tokens, width = qkv.shape
    rows, columns = w_out.shape
    cols = columns // 8
    dma = pltpu.SemaphoreType.DMA
    halves = pl.pallas_call(
        kernel,
        out_shape=jax.ShapeDtypeStruct((2, tokens, columns), BF),
        in_specs=[
            pl.BlockSpec(memory_space=pltpu.SMEM),
            pl.BlockSpec(memory_space=pl.ANY),
            pl.BlockSpec(memory_space=pl.ANY),
        ],
        out_specs=pl.BlockSpec(memory_space=pl.ANY),
        scratch_shapes=[
            pltpu.VMEM((3, 2, 16, width), BF),
            pltpu.VMEM((2, 2, 256, 128), BF),
            pltpu.VMEM((2, 2, 8, 2, 256, 128), BF),
            pltpu.VMEM((NZ, 2, rows, cols), BF),
            pltpu.VMEM((4, 256, 128), F32),
            pltpu.VMEM((4, 256, 256), F32),
            pltpu.VMEM((2, 2, NZ, 2, 16, 128), BF),
            pltpu.VMEM((8, 2, 2, 16, 2048), BF),
            pltpu.VMEM((16, 32, cols), BF),
            dma((2,)), dma((3,)), dma((3,)), dma((2, 2, 7)), dma((2, 2, 7)), dma((15,)), dma((15,)),
            dma((2,)), dma((2,)), dma((2, 10)), dma((2, 10)), dma, dma,
        ],
        compiler_params=pltpu.CompilerParams(
            collective_id=0, has_side_effects=True, vmem_limit_bytes=66_400_000
        ),
        name="attend_and_project",
    )(frame_clip, qkv.reshape(parts, 2, tokens // 2, width), w_out)
    return (halves[0].astype(F32) + halves[1].astype(F32)).astype(BF)


def solution(mesh):
    in_specs = (P(None, ("blk", "tile"), None), P(), P("tile", None))
    out_specs = P(("blk", "tile"), None)
    return jax.shard_map(
        on_device, mesh=mesh, in_specs=in_specs, out_specs=out_specs, check_vma=False
    )
```

```python
import functools
import math

import jax
import jax.numpy as jnp
from jax import lax
from jax.experimental import pallas as pl
from jax.experimental.pallas import tpu as pltpu
from jax.sharding import PartitionSpec as P

MESH = pl.DeviceIdType.MESH
BF = jnp.bfloat16
F32 = jnp.float32
NEG = -1e30
NX, NY, NZ = 4, 4, 8


def place():
    b = lax.axis_index("blk")
    t = lax.axis_index("tile")
    return b % NX, b // NX, t // 16, (t // 2) % NZ, t % 2


def dev(x, y, z, c):
    return {"blk": (y % 2) * NX + x, "tile": (y // 2) * 16 + z * 2 + c}


def kernel(
    clip_ref, qkv_ref, w_in, pr,
    src, q_ref, kv, w_ref, m_ref, acc_ref, o_ref, oa, ps,
    lsem, a_send, a_recv, kv_send, kv_recv, w_send, w_recv,
    o_send, o_recv, oa_send, oa_recv, p_send, p_recv,
):
    x, ylo, yhi, z, c = place()
    y = yhi * 2 + ylo
    yp = NY - 1 - y
    sib = 1 - c
    cols = w_ref.shape[-1]
    coef = math.log2(math.e) / math.sqrt(128)

    def remote(s, d, ss, rs, device):
        return pltpu.make_async_remote_copy(
            src_ref=s, dst_ref=d, send_sem=ss, recv_sem=rs, device_id=device, device_id_type=MESH
        )

    def hop(k):
        return jnp.where(k % 2 == 0, k // 2, NZ - (k + 1) // 2)

    def plane(n):
        return (y + n % NY) % NY, (z + hop(n // NY)) % NZ

    def column(yy, zz):
        return pl.multiple_of(((yy // 2) * 16 + zz * 2 + yy % 2) * 128, 128)

    load = pltpu.make_async_copy(qkv_ref, src, lsem.at[0])
    load.start()

    barrier = pltpu.get_barrier_semaphore()

    def greet(device):
        pl.semaphore_signal(barrier, inc=1, device_id=device, device_id_type=MESH)

    def greet_plane(n, carry):
        yy, zz = plane(n)
        greet(dev(x, yy, zz, c))
        return carry

    lax.fori_loop(1, NY * NZ, greet_plane, 0)
    greet(dev(x, y, z, sib))
    greet(dev(x, yp, z, sib))

    def greet_line(n, carry):
        xx = (x + n) % NX
        greet(dev(xx, y, z, c))
        greet(dev(xx, y, z, sib))
        greet(dev(xx, yp, z, c))
        greet(dev(xx, yp, z, sib))
        return carry

    lax.fori_loop(1, NX, greet_line, 0)
    load.wait()
    pl.semaphore_wait(barrier, NY * NZ - 1 + 2 + 4 * (NX - 1))

    row = pl.multiple_of((yhi * NZ + z) * 16, 16)

    def cut(k, column):
        if k == 2:
            return src.at[0, :, :, pl.ds(column, 128)]
        return src.at[1:3, k, :, pl.ds(column, 128)]

    def landing(k):
        if k == 2:
            return q_ref.at[ylo, :, pl.ds(row, 16), :]
        return kv.at[:, ylo, 2 * x + k, c, pl.ds(row, 16), :]

    def scatter(k):
        def send(n, carry):
            yy, zz = plane(NY * NZ - n)
            remote(
                cut(k, column(yy, zz)), landing(k), a_send.at[k], a_recv.at[k],
                dev(x, yy, zz, c),
            ).start()
            return carry

        pltpu.make_async_copy(cut(k, column(y, z)), landing(k), a_recv.at[k]).start()
        lax.fori_loop(1, NY * NZ, send, 0)

    scatter(0)
    scatter(2)
    scatter(1)

    def wcols(core):
        return pl.ds(pl.multiple_of((x * 2 + core) * cols, 128), cols)

    w_own = pltpu.make_async_copy(w_in.at[:, wcols(c)], w_ref.at[z, c], lsem.at[1])
    w_own.start()
    w_sib = remote(
        w_in.at[:, wcols(sib)], w_ref.at[z, c], w_send.at[0], w_recv.at[0], dev(x, y, z, sib)
    )
    w_sib.start()

    def piece(k, i, r, core):
        return kv.at[k, :, 2 * ((x - r + NX) % NX) + i, core]

    def spread(k, i, r, slot, device):
        remote(
            piece(k, i, r, c), piece(k, i, r, c), kv_send.at[k, i, slot], kv_recv.at[k, i, slot],
            device,
        ).start()

    def share(k, i, r):
        spread(k, i, r, 3 + r, dev(x, y, z, sib))

    def arrived(k, i, r, core, slot):
        spot = piece(k, i, r, core)
        pltpu.make_async_copy(spot, spot, kv_recv.at[k, i, slot]).wait()

    right, left = dev((x + 1) % NX, y, z, c), dev((x + NX - 1) % NX, y, z, c)

    def neighbours(i):
        own = kv.at[:, :, 2 * x + i, c]
        pltpu.make_async_copy(own, own, a_recv.at[i]).wait()
        for k in range(2):
            spread(k, i, 0, 0, right)
            spread(k, i, 0, 2, left)
            share(k, i, 0)

    def relay(i):
        arrived(0, i, 1, c, 0)
        spread(0, i, 1, 1, right)
        share(0, i, 1)
        arrived(1, i, 3, c, 2)
        spread(1, i, 3, 1, left)
        share(1, i, 3)
        arrived(0, i, 3, c, 2)
        share(0, i, 3)
        arrived(1, i, 1, c, 0)
        share(1, i, 1)

    def far(i):
        for k in range(2):
            arrived(k, i, 2, c, 1)
            share(k, i, 2)

    def other(i, r):
        for k in range(2):
            arrived(k, i, r, sib, 3 + r)

    w_own.wait()
    w_sib.wait_recv()
    twin = dev(x, yhi * 2 + 1 - ylo, z, c)

    def w_copy(block, half, slot, device):
        spot = w_ref.at[block, half]
        remote(spot, spot, w_send.at[slot], w_recv.at[slot], device).start()

    def w_wait(block, half, slot):
        spot = w_ref.at[block, half]
        pltpu.make_async_copy(spot, spot, w_recv.at[slot]).wait()

    def above(s):
        return (z + s) % NZ

    def below(s):
        return (z - s + NZ) % NZ

    def forward(s):
        if s:
            w_wait(below(s), ylo, s)
            w_copy(below(s), ylo, 7 + s, twin)
            if s < 4:
                w_wait(above(s), ylo, 4 + s)
                w_copy(above(s), ylo, 11 + s, twin)
        if s < 4:
            w_copy(below(s), ylo, 1 + s, dev(x, y, above(1), c))
        if s < 3:
            w_copy(above(s), ylo, 5 + s, dev(x, y, below(1), c))

    def w_finish():
        for s in range(1, 5):
            w_wait(below(s), 1 - ylo, 7 + s)
            if s < 4:
                w_wait(above(s), 1 - ylo, 11 + s)

    neighbours(0)
    forward(0)
    relay(0)
    pltpu.make_async_copy(q_ref, q_ref, a_recv.at[2]).wait()

    m_ref[...] = jnp.full_like(m_ref, NEG)
    acc_ref[...] = jnp.zeros_like(acc_ref)

    def block(xs, i, js):
        g = 2 * xs + i
        keys = jnp.concatenate([kv[0, half, g].reshape(512, 128) for half in range(2)], axis=0)
        values = jnp.concatenate([kv[1, half, g].reshape(512, 128) for half in range(2)], axis=0)
        values = jnp.concatenate([values, jnp.ones_like(values)], axis=1)
        for j in js:
            query_clip = clip_ref[(j // 2) * 8 + 2 * x + j % 2]
            kept = [query_clip == clip_ref[half * 8 + g] for half in range(2)]
            s = lax.dot_general(
                q_ref[j // 2, j % 2], keys, (((1,), (1,)), ((), ())),
                preferred_element_type=F32,
            )
            s = [s[:, :512], s[:, 512:]]
            tops = [
                jnp.where(kept[half], jnp.max(s[half], axis=1, keepdims=True), NEG)
                for half in range(2)
            ]
            old = m_ref[j]
            new = jnp.maximum(old, jnp.maximum(tops[0], tops[1]) * coef)
            alpha = jnp.exp2(old - new)
            m_ref[j] = new
            p = [
                jnp.exp2(s[half] * coef - jnp.where(kept[half], new, -NEG)[:, :1]).astype(BF)
                for half in range(2)
            ]
            acc_ref[j] = acc_ref[j] * jnp.concatenate([alpha, alpha], axis=1) + jnp.dot(
                jnp.concatenate(p, axis=1), values, preferred_element_type=F32
            )

    order = ((0, 0), (1, 0), (3, 0), (0, 1), (2, 0), (1, 1), (3, 1), (2, 1))

    def pick(step, table):
        value = table[0]
        for n in range(1, len(table)):
            value = jnp.where(step == n, table[n], value)
        return value

    def attend(step, carry):
        @pl.when(step == 0)
        def _():
            other(0, 0)

        @pl.when(step == 1)
        def _():
            other(0, 1)

        @pl.when(step == 2)
        def _():
            other(0, 3)
            neighbours(1)

        @pl.when(step == 3)
        def _():
            far(0)
            other(1, 0)
            forward(1)

        @pl.when(step == 4)
        def _():
            other(0, 2)

        @pl.when(step == 5)
        def _():
            relay(1)
            other(1, 1)
            forward(2)

        @pl.when(step == 6)
        def _():
            other(1, 3)

        r = pick(step, [pair[0] for pair in order])
        block((x - r + NX) % NX, pick(step, [pair[1] for pair in order]), range(4))
        return carry

    lax.fori_loop(0, 7, attend, 0)
    far(1)
    other(1, 2)

    me = x * 2 + c
    mine = ylo ^ yhi
    head = pl.multiple_of((z * 2 + ylo) * 128, 128)

    def o_move(half):
        def go(n, carry):
            n = 2 * NZ - n
            pair = (mine + n % 2) % 2
            zz = (z + hop(n // 2)) % NZ
            remote(
                o_ref.at[half, pair, zz], oa.at[me, pair ^ half, :, :, pl.ds(head, 128)],
                o_send.at[half], o_recv.at[half], dev(x, yhi * 2 + (pair ^ yhi), zz, c),
            ).start()
            return carry

        for i in range(2):
            acc = acc_ref[2 * half + i]
            o = (acc[:, :128] / acc[:, 128:]).astype(BF)
            for yh in range(2):
                o_ref[half, half ^ yh, :, i] = o[yh * 128:(yh + 1) * 128].reshape(NZ, 16, 128)
        pltpu.make_async_copy(
            o_ref.at[half, mine, z], oa.at[me, mine ^ half, :, :, pl.ds(head, 128)],
            o_recv.at[half],
        ).start()
        lax.fori_loop(1, 2 * NZ, go, 0)

    for half in range(2):
        block((x - 2 + NX) % NX, 1, (2 * half, 2 * half + 1))
        o_move(half)
    forward(3)

    def oa_spot(half, r, core, i=None):
        spot = oa.at[((x - r + NX) % NX) * 2 + core, mine ^ half]
        return spot if i is None else spot.at[i]

    def oa_copy(half, r, i, slot, device):
        spot = oa_spot(half, r, c, i)
        remote(spot, spot, oa_send.at[half, slot], oa_recv.at[half, slot], device).start()

    def oa_arrived(half, r, core, i, slot):
        spot = oa_spot(half, r, core, i)
        pltpu.make_async_copy(spot, spot, oa_recv.at[half, slot]).wait()

    def oa_share(half, r):
        oa_copy(half, r, None, 6 + r, dev(x, y, z, sib))

    for half in range(2):
        own = oa_spot(half, 0, c)
        pltpu.make_async_copy(own, own, o_recv.at[half]).wait()
        for i in range(2):
            oa_copy(half, 0, i, 3 * i, right)
            oa_copy(half, 0, i, 3 * i + 2, left)
        oa_share(half, 0)
    for half in range(2):
        oa_arrived(half, 1, c, 0, 0)
        oa_copy(half, 1, 0, 1, right)
        oa_arrived(half, 3, c, 1, 5)
        oa_copy(half, 3, 1, 4, left)
        oa_arrived(half, 1, c, 1, 3)
        oa_share(half, 1)
        oa_arrived(half, 3, c, 0, 2)
        oa_share(half, 3)
    forward(4)
    for half in range(2):
        oa_arrived(half, 2, c, 0, 1)
        oa_arrived(half, 2, c, 1, 4)
        oa_share(half, 2)
    w_finish()

    for half in range(2):
        for r in range(NX):
            oa_arrived(half, r, sib, None, 6 + r)
        h = mine ^ half
        part = jnp.dot(
            oa[:, h].reshape(256, 2048), w_ref[...].reshape(2048, cols),
            preferred_element_type=F32,
        )
        ps[pl.ds(8 * half, 8)] = part.astype(BF).reshape(8, 32, cols)
        land = pr.at[yhi, :, wcols(c)]

        def deliver(n, carry, half=half, h=h, land=land):
            n = 7 - n
            xx = (x + n // 2) % NX
            core = (c + n) % 2
            spot = ps.at[8 * half + 2 * xx + core]
            here = jnp.logical_and(n == 0, h == yhi)

            @pl.when(here)
            def _():
                pltpu.make_async_copy(spot, land, p_recv).start()

            @pl.when(jnp.logical_not(here))
            def _():
                remote(
                    spot, land, p_send, p_recv, dev(xx, h * 2 + (mine ^ h), z, core)
                ).start()

            return carry

        lax.fori_loop(0, 8, deliver, 0)
    pltpu.make_async_copy(pr, pr, p_recv).wait()

    def left_here(spot, sem):
        pltpu.make_async_copy(spot, spot, sem).wait()

    for k in range(3):
        left_here(src.at[0, :, :, pl.ds(0, (NY * NZ - 1) * 128)], a_send.at[k])
    left_here(w_ref.at[z, c], w_send.at[0])
    for slot in range(1, 15):
        left_here(w_ref.at[z, ylo], w_send.at[slot])
    for k in range(2):
        for i in range(2):
            for slot in range(7):
                left_here(piece(k, i, 0, c), kv_send.at[k, i, slot])
    for half in range(2):
        left_here(oa.at[0, 0, :, :, pl.ds(0, (2 * NZ - 1) * 128)], o_send.at[half])
        for slot in range(10):
            left_here(oa_spot(half, 0, c, 0 if slot < 6 else None), oa_send.at[half, slot])
    sent = ps.at[pl.ds(0, 15)]
    pltpu.make_async_copy(sent, sent, p_send).wait()


def on_device(qkv, frame_clip, w_out):
    parts, tokens, width = qkv.shape
    rows, columns = w_out.shape
    cols = columns // 8
    dma = pltpu.SemaphoreType.DMA
    halves = pl.pallas_call(
        kernel,
        out_shape=jax.ShapeDtypeStruct((2, tokens, columns), BF),
        in_specs=[
            pl.BlockSpec(memory_space=pltpu.SMEM),
            pl.BlockSpec(memory_space=pl.ANY),
            pl.BlockSpec(memory_space=pl.ANY),
        ],
        out_specs=pl.BlockSpec(memory_space=pl.ANY),
        scratch_shapes=[
            pltpu.VMEM((3, 2, 16, width), BF),
            pltpu.VMEM((2, 2, 256, 128), BF),
            pltpu.VMEM((2, 2, 8, 2, 256, 128), BF),
            pltpu.VMEM((NZ, 2, rows, cols), BF),
            pltpu.VMEM((4, 256, 128), F32),
            pltpu.VMEM((4, 256, 256), F32),
            pltpu.VMEM((2, 2, NZ, 2, 16, 128), BF),
            pltpu.VMEM((8, 2, 2, 16, 2048), BF),
            pltpu.VMEM((16, 32, cols), BF),
            dma((2,)), dma((3,)), dma((3,)), dma((2, 2, 7)), dma((2, 2, 7)), dma((15,)), dma((15,)),
            dma((2,)), dma((2,)), dma((2, 10)), dma((2, 10)), dma, dma,
        ],
        compiler_params=pltpu.CompilerParams(
            collective_id=0, has_side_effects=True, vmem_limit_bytes=66_400_000
        ),
        name="attend_and_project",
    )(frame_clip, qkv.reshape(parts, 2, tokens // 2, width), w_out)
    return (halves[0].astype(F32) + halves[1].astype(F32)).astype(BF)


def solution(mesh):
    in_specs = (P(None, ("blk", "tile"), None), P(), P("tile", None))
    out_specs = P(("blk", "tile"), None)
    return jax.shard_map(
        on_device, mesh=mesh, in_specs=in_specs, out_specs=out_specs, check_vma=False
    )
```
